256 devices in a mesh: row: 8 (over z), col: 32 (over y, x, core).
Axes of the slice: x: 4, y: 4, z: 8, core: 2. Of those that a mesh axis runs over, the one named last changes fastest.
Arguments:
- panel_block: bfloat16 [28672, 1024], P(('row', 'col')), may hold values from -1.5 to 1.5
- diag_inverse: bfloat16 [2, 512, 512], replicated
- trailing: bfloat16 [28672, 28672], P('row', 'col'), may hold values from -6 to 6
Outputs:
- factor_panel: bfloat16 [28672, 1024], P(('row', 'col'))
- updated: bfloat16 [28672, 28672], P('row', 'col')
The draws below stay inside these ranges and needn't reach their ends.
All inputs are finite; a program needn't handle non-finite values.
Results may differ from the reference program's by a relative error of at most 0.0054.
Values may be sent and summed in bfloat16 or wider, within the bound.
A program may use at most 128 MiB of HBM per device.

```python
import math
import jax
import jax.numpy as jnp
from jax import lax

NB = 512
PANELS = 2
CH = 112
RB = 3584
M = 28672
N_ROW = 8
N_COL = 32


def draw_diag_inverse(key, part):
    first_key, second_key, third_key = jax.random.split(key, 3)
    spread_size = 0.35 / math.sqrt(NB)
    entries = jnp.clip(jax.random.normal(first_key, (PANELS, NB, NB), jnp.float32), -4.0, 4.0)
    diagonal_values = 0.8 + 0.45 * jax.random.uniform(second_key, (PANELS, NB), jnp.float32)
    top_place = jax.random.randint(third_key, (PANELS, 1), 0, NB)
    positions = lax.broadcasted_iota(jnp.int32, (PANELS, NB), 1)
    diagonal_values = jnp.where(positions == top_place, 1.25, diagonal_values)
    identity = jnp.eye(NB, dtype=jnp.float32)
    matrix = entries * spread_size * (1.0 - identity) + identity * diagonal_values[:, :, None]
    return matrix.astype(jnp.bfloat16)


def steps_of(key, extent, shards, low, top_value):
    loudness, own = 1.0, jax.random.fold_in(key, 6)
    for position, shards_of in shards:
        heights = jnp.exp(jax.random.uniform(jax.random.fold_in(own, position), (shards_of,), jnp.float32, low / len(shards), top_value / len(shards)))
        loudness = loudness * jnp.repeat(heights, extent[position] // shards_of).reshape([-1 if axis == position else 1 for axis in range(len(extent))])
    return loudness


def centred(own_key, dims, deviation, limit, cuts=(), held_as=jnp.bfloat16):
    values = jax.random.normal(own_key, dims, jnp.float32) * deviation
    if len(cuts) > 0:
        values = steps_of(own_key, dims, cuts, -0.22, 0.18) * values
    return jnp.clip(values, min=-limit, max=limit).astype(held_as)


def setup_inputs(seed: int = 0) -> dict:
    key_of = jax.random.split(jax.random.key(seed), 4)
    panel_block = centred(key_of[0], (M, PANELS * NB), 0.25, 1.5, ((0, 256),))
    diag_inverse = draw_diag_inverse(jax.random.fold_in(key_of[3], 71), 0)
    trailing = centred(key_of[2], (M, M), 1.0, 6.0, ((0, 8), (1, 32)))
    return dict(panel_block=panel_block, diag_inverse=diag_inverse, trailing=trailing)


def reference(panel_block, diag_inverse, trailing):
    pieces = []
    for panel in range(PANELS):
        columns = panel_block[:, panel * NB:(panel + 1) * NB]
        pieces.append(jnp.dot(columns, jnp.tril(diag_inverse[panel]).T, preferred_element_type=jnp.float32).astype(jnp.bfloat16))
    factor = jnp.concatenate(pieces, axis=1)
    width = PANELS * NB
    column_factor = factor.reshape(N_ROW, N_COL, CH, width).transpose(1, 0, 2, 3).reshape(N_ROW * N_COL * CH, width)
    right_side = column_factor.astype(jnp.float32)

    def one_block(index):
        start = (index * RB).astype(jnp.int32)
        left_rows = lax.dynamic_slice_in_dim(factor, start, RB, 0).astype(jnp.float32)
        previous = lax.dynamic_slice_in_dim(trailing, start, RB, 0).astype(jnp.float32)
        product = jnp.dot(left_rows, right_side.T, precision=lax.Precision.HIGHEST)
        return (previous - product).astype(jnp.bfloat16)

    blocks = lax.map(one_block, jnp.arange(N_ROW).astype(jnp.int32))
    return factor, blocks.reshape(N_ROW * RB, N_ROW * N_COL * CH)
```

```python
import jax
import jax.numpy as jnp
from jax import lax
from jax.experimental import pallas as pl
from jax.experimental.pallas import tpu as pltpu
from jax.sharding import PartitionSpec as P

NB = 512
CH = 112
NZ = 8
NY = 4
NX = 4
PAIR = 2 * CH
COLS = NZ * CH
ROWS = NY * NX * PAIR
QUARTER = NB // 2
MESH = pl.DeviceIdType.MESH
NT = (((1,), (1,)), ((), ()))

RECV = [
    [(0, 0, -1), (1, -1, 0), (0, 0, 1), (1, 1, 0)],
    [(1, 0, -1), (0, -1, 0), (1, 0, 1), (0, 1, 0)],
    [(0, 0, 2), (1, 2, 0), (0, 1, -1), (1, -1, 1)],
    [(0, -1, -1), (1, -1, -1), (0, 1, 1), (1, 1, 1)],
    [(0, -1, 1), (1, 1, -1), (0, 1, 2), (1, 2, 1)],
    [(0, 2, 0), (1, 0, 2), (0, 2, -1), (1, -1, 2)],
    [(0, -1, 2), (1, 2, -1), (0, 2, 2), (1, 2, 2)],
    [(0, 2, 1), (1, 1, 2)],
]
ZPARTS = [(0, 0, NB), (1, 0, QUARTER), (1, QUARTER, QUARTER)]


def place():
    j = lax.axis_index("col")
    return lax.axis_index("row"), lax.div(j, 8), lax.rem(lax.div(j, 2), NX), lax.rem(j, 2)


def forwards(chunk):
    panel, dy, dx = chunk
    near, far = (dx, dy) if panel == 0 else (dy, dx)
    steps = []
    if far == 0:
        if near == 0:
            steps += [("near", 1), ("near", -1)]
        elif near == -1:
            steps += [("near", 1)]
        steps += [("far", 1), ("far", -1)]
    elif far == -1 and near in (0, 1):
        steps += [("far", 1)]
    elif far == 1 and near in (-1, 2):
        steps += [("far", -1)]
    axis = {"near": 1 - panel, "far": panel}
    return [(0, d) if axis[kind] == 1 else (d, 0) for kind, d in steps]


def gather_kernel(panel_hbm, diag_hbm, ra, rb, c0, c1, c2, pv, dv, lsem, ssem, rsem, zsem):
    z, y, x, c = place()
    sign = 1 - 2 * c
    rows = (ra, rb)
    cols = (c0, c1, c2)

    def device(dz, dy, dx, dc):
        zz = lax.rem(z + sign * dz + NZ, NZ)
        yy = lax.rem(y + sign * dy + NY, NY)
        xx = lax.rem(x + sign * dx + NX, NX)
        cc = 1 - c if dc else c
        return (zz, (yy * NX + xx) * 2 + cc)

    loads = [
        pltpu.make_async_copy(panel_hbm, pv, lsem.at[0]),
        pltpu.make_async_copy(diag_hbm, dv, lsem.at[1]),
    ]
    for load in loads:
        load.start()
    barrier = pltpu.get_barrier_semaphore()
    around = [(1, 0, 0, 0), (-1, 0, 0, 0), (0, 1, 0, 0), (0, -1, 0, 0), (0, 0, 1, 0), (0, 0, -1, 0), (0, 0, 0, 1)]
    for offset in around:
        pl.semaphore_signal(barrier, inc=1, device_id=device(*offset), device_id_type=MESH)
    for load in loads:
        load.wait()

    mine = pl.ds(pl.multiple_of(c * CH, 16), CH)
    own = pl.ds(pl.multiple_of(z * CH, 16), CH)
    below = lax.broadcasted_iota(jnp.int32, (NB, NB), 0) >= lax.broadcasted_iota(jnp.int32, (NB, NB), 1)
    for panel in range(2):
        full = dv[panel].astype(jnp.float32)
        lower = jnp.where(below, full, 0.0).astype(jnp.bfloat16)
        block = lax.dot_general(
            pv[:, panel * NB : (panel + 1) * NB], lower, NT, preferred_element_type=jnp.float32
        ).astype(jnp.bfloat16)
        rows[panel][y, x, mine, :] = block
        for part, (of, first, width) in enumerate(ZPARTS):
            if of == panel:
                cols[part][own, :] = block[:, first : first + width]
    pl.semaphore_wait(barrier, len(around))

    sent = []

    def send(ref, recv_sem, offset):
        copy = pltpu.make_async_remote_copy(
            src_ref=ref,
            dst_ref=ref,
            send_sem=ssem.at[len(sent)],
            recv_sem=recv_sem,
            device_id=device(*offset),
            device_id_type=MESH,
        )
        copy.start()
        sent.append(copy)

    def slot(chunk, mirrored=False):
        panel, dy, dx = chunk
        way, core = (-sign, 1 - c) if mirrored else (sign, c)
        yy = lax.rem(y + way * dy + NY, NY)
        xx = lax.rem(x + way * dx + NX, NX)
        ref = rows[panel].at[yy, xx, pl.ds(pl.multiple_of(core * CH, 16), CH), :]
        return ref, rsem.at[panel * 32 + (yy * NX + xx) * 2 + core]

    def wait(ref, sem):
        pltpu.make_async_remote_copy(
            src_ref=ref, dst_ref=ref, send_sem=ssem.at[0], recv_sem=sem, device_id=device(0, 0, 0, 1), device_id_type=MESH
        ).wait_recv()

    def pass_on(chunk):
        ref, sem = slot(chunk)
        for dy, dx in forwards(chunk):
            send(ref, sem, (0, dy, dx, 0))
        send(ref, sem, (0, 0, 0, 1))

    def zslot(part, dz):
        zz = lax.rem(z + sign * dz + NZ, NZ)
        return cols[part].at[pl.ds(pl.multiple_of(zz * CH, 16), CH), :], zsem.at[part * NZ + zz]

    def zsend(part, dz, way):
        ref, sem = zslot(part, dz)
        send(ref, sem, (way, 0, 0, 0))

    def zround(part, hop):
        for way in (1, -1):
            if hop == NZ // 2 and way != (1 if part == 0 else -1):
                continue
            ref, sem = zslot(part, -way * hop)
            wait(ref, sem)
            if hop + 1 < NZ // 2 or (hop + 1 == NZ // 2 and way == (1 if part == 0 else -1)):
                send(ref, sem, (way, 0, 0, 0))

    zorder = [(part, hop) for hop in range(1, NZ // 2 + 1) for part in range(len(ZPARTS))]
    for part in range(len(ZPARTS)):
        if part == 0:
            pass_on((0, 0, 0))
        if part == 1:
            pass_on((1, 0, 0))
        for way in (1, -1):
            zsend(part, 0, way)
    done = 0
    for step, chunks in enumerate(RECV):
        for chunk in chunks:
            wait(*slot(chunk))
            pass_on(chunk)
        upto = ZSTEPS[step]
        for part, hop in zorder[done:upto]:
            zround(part, hop)
        done = upto
    for chunks in [[(0, 0, 0), (1, 0, 0)]] + RECV:
        for chunk in chunks:
            wait(*slot(chunk, mirrored=True))
    for copy in sent:
        copy.wait_send()


ZSTEPS = [1, 3, 4, 6, 7, 9, 12, 12]
N_SENDS = 30 + 32 + 7 * len(ZPARTS)
TILE = 448


def update_kernel(ra, rb, c0, c1, c2, t_hbm, f_hbm, o_hbm, tb, ob, tsem, osem, fsem):
    _, y, x, c = place()
    mine = pl.ds(pl.multiple_of(c * CH, 16), CH)
    keep = [
        pltpu.make_async_copy(r.at[y, x, mine, :], f_hbm.at[:, panel * NB : (panel + 1) * NB], fsem.at[panel])
        for panel, r in enumerate((ra, rb))
    ]
    steps = ROWS // TILE
    pairs = TILE // PAIR

    def read(i, s):
        return pltpu.make_async_copy(t_hbm.at[pl.ds(pl.multiple_of(i * TILE, 64), TILE)], tb.at[s], tsem.at[s])

    def write(i, s):
        return pltpu.make_async_copy(ob.at[s], o_hbm.at[pl.ds(pl.multiple_of(i * TILE, 64), TILE)], osem.at[s])

    read(0, 0).start()
    read(1, 1).start()
    for copy in keep:
        copy.start()

    def step(i, _):
        s = lax.rem(i, 2)
        read(i, s).wait()
        yy = lax.div(i, NX // pairs)
        xx = pl.ds(lax.rem(i, NX // pairs) * pairs, pairs)
        left = ra[yy, xx].reshape(TILE, NB)
        right = rb[yy, xx].reshape(TILE, NB)
        product = lax.dot_general(left, c0[...], NT, preferred_element_type=jnp.float32)
        product += lax.dot_general(right[:, :QUARTER], c1[...], NT, preferred_element_type=jnp.float32)
        product += lax.dot_general(right[:, QUARTER:], c2[...], NT, preferred_element_type=jnp.float32)

        @pl.when(i >= 2)
        def _():
            write(i - 2, s).wait()

        ob[s] = (tb[s].astype(jnp.float32) - product).astype(jnp.bfloat16)
        write(i, s).start()

        @pl.when(i + 2 < steps)
        def _():
            read(i + 2, s).start()

        return 0

    lax.fori_loop(0, steps, step, 0)
    write(steps - 2, steps % 2).wait()
    write(steps - 1, (steps - 1) % 2).wait()
    for copy in keep:
        copy.wait()


def body(panel_block, diag_inverse, trailing):
    vmem = pl.BlockSpec(memory_space=pltpu.VMEM)
    hbm = pl.BlockSpec(memory_space=pltpu.HBM)
    bf16 = jnp.bfloat16
    half = jax.ShapeDtypeStruct((NY, NX, PAIR, NB), bf16)
    gathered = pl.pallas_call(
        gather_kernel,
        name="gather",
        out_shape=[half, half] + [jax.ShapeDtypeStruct((COLS, width), bf16) for _, _, width in ZPARTS],
        in_specs=[hbm] * 2,
        out_specs=[vmem] * (2 + len(ZPARTS)),
        scratch_shapes=[
            pltpu.VMEM((CH, 2 * NB), bf16),
            pltpu.VMEM((2, NB, NB), bf16),
            pltpu.SemaphoreType.DMA((2,)),
            pltpu.SemaphoreType.DMA((N_SENDS,)),
            pltpu.SemaphoreType.DMA((64,)),
            pltpu.SemaphoreType.DMA((NZ * len(ZPARTS),)),
        ],
        compiler_params=pltpu.CompilerParams(
            collective_id=0, has_side_effects=True, vmem_limit_bytes=24 << 20
        ),
    )(*(pltpu.with_memory_space_constraint(a, pltpu.HBM) for a in (panel_block, diag_inverse)))
    return pl.pallas_call(
        update_kernel,
        name="update",
        out_shape=[
            jax.ShapeDtypeStruct(panel_block.shape, bf16),
            jax.ShapeDtypeStruct(trailing.shape, bf16),
        ],
        in_specs=[vmem] * len(gathered) + [hbm],
        out_specs=[hbm] * 2,
        scratch_shapes=[
            pltpu.VMEM((2, TILE, COLS), bf16),
            pltpu.VMEM((2, TILE, COLS), bf16),
            pltpu.SemaphoreType.DMA((2,)),
            pltpu.SemaphoreType.DMA((2,)),
            pltpu.SemaphoreType.DMA((2,)),
        ],
        compiler_params=pltpu.CompilerParams(vmem_limit_bytes=24 << 20),
    )(*gathered, pltpu.with_memory_space_constraint(trailing, pltpu.HBM))


def solution(mesh):
    placed = (P(("row", "col"), None), P(), P("row", "col"))
    return jax.shard_map(
        body,
        mesh=mesh,
        in_specs=placed,
        out_specs=(P(("row", "col"), None), P("row", "col")),
        check_vma=False,
    )
```

```python
import jax
import jax.numpy as jnp
from jax import lax
from jax.experimental import pallas as pl
from jax.experimental.pallas import tpu as pltpu
from jax.sharding import PartitionSpec as P

NB = 512
CH = 112
NZ = 8
NY = 4
NX = 4
PAIR = 2 * CH
COLS = NZ * CH
ROWS = NY * NX * PAIR
QUARTER = NB // 2
MESH = pl.DeviceIdType.MESH
NT = (((1,), (1,)), ((), ()))

RECV = [
    [(0, 0, -1), (1, -1, 0), (0, 0, 1), (1, 1, 0)],
    [(1, 0, -1), (0, -1, 0), (1, 0, 1), (0, 1, 0)],
    [(0, 0, 2), (1, 2, 0), (0, 1, -1), (1, -1, 1)],
    [(0, -1, -1), (1, -1, -1), (0, 1, 1), (1, 1, 1)],
    [(0, -1, 1), (1, 1, -1), (0, 1, 2), (1, 2, 1)],
    [(0, 2, 0), (1, 0, 2), (0, 2, -1), (1, -1, 2)],
    [(0, -1, 2), (1, 2, -1), (0, 2, 2), (1, 2, 2)],
    [(0, 2, 1), (1, 1, 2)],
]
ZPARTS = [(0, 0), (0, QUARTER), (1, 0), (1, QUARTER)]
PLAN = [
    ("own", 3),
    ("z", 0, 1),
    ("z", 1, 1),
    ("row", 0),
    ("z", 2, 1),
    ("z", 3, 1),
    ("row", 1),
    ("z", 0, 2),
    ("z", 1, 2),
    ("row", 2),
    ("z", 2, 2),
    ("z", 3, 2),
    ("row", 3),
    ("z", 0, 3),
    ("z", 1, 3),
    ("row", 4),
    ("z", 2, 3),
    ("z", 3, 3),
    ("row", 5),
    ("z", 0, 4),
    ("z", 1, 4),
    ("do", 0, [(0, -1), (0, 0), (0, 1), (0, 2)]),
    ("row", 6),
    ("do", 0, [(1, -1), (1, 0), (1, 1)]),
    ("do", 0, [(-1, -1), (-1, 0), (-1, 1)]),
    ("z", 2, 4),
    ("z", 3, 4),
    ("row", 7),
    ("do", 0, [(1, 2), (-1, 2), (2, 0), (2, 2)]),
    ("do", 1, [(-1, 0), (0, 0), (1, 0), (2, 0)]),
    ("do", 1, [(-1, -1), (0, -1), (1, -1)]),
    ("do", 1, [(-1, 1), (0, 1), (1, 1)]),
]
DONE = {(step[1], chip) for step in PLAN if step[0] == "do" for chip in step[2]}
CHIPS = [(dy, dx) for dy in (2, -1, 0, 1) for dx in (-1, 1, 0, 2)]
UNTOUCHED = [chip for chip in CHIPS if (0, chip) not in DONE and (1, chip) not in DONE]


def place():
    j = lax.axis_index("col")
    return lax.axis_index("row"), lax.div(j, 8), lax.rem(lax.div(j, 2), NX), lax.rem(j, 2)


def forwards(chunk):
    panel, dy, dx = chunk
    near, far = (dx, dy) if panel == 0 else (dy, dx)
    steps = []
    if far == 0:
        if near == 0:
            steps += [("near", 1), ("near", -1)]
        elif near == -1:
            steps += [("near", 1)]
        steps += [("far", 1), ("far", -1)]
    elif far == -1 and near in (0, 1):
        steps += [("far", 1)]
    elif far == 1 and near in (-1, 2):
        steps += [("far", -1)]
    axis = {"near": 1 - panel, "far": panel}
    return [(0, d) if axis[kind] == 1 else (d, 0) for kind, d in steps]


def gather_kernel(panel_hbm, diag_hbm, t_hbm, ra, rb, ca, cb, acc, pv, dv, tv, lsem, ssem, rsem, zsem):
    z, y, x, c = place()
    sign = 1 - 2 * c
    rows = (ra, rb)
    cols = (ca, cb)

    def device(dz, dy, dx, dc):
        zz = lax.rem(z + sign * dz + NZ, NZ)
        yy = lax.rem(y + sign * dy + NY, NY)
        xx = lax.rem(x + sign * dx + NX, NX)
        cc = 1 - c if dc else c
        return (zz, (yy * NX + xx) * 2 + cc)

    loads = [
        pltpu.make_async_copy(panel_hbm, pv, lsem.at[0]),
        pltpu.make_async_copy(diag_hbm.at[0], dv.at[0], lsem.at[1]),
        pltpu.make_async_copy(diag_hbm.at[1], dv.at[1], lsem.at[2]),
        pltpu.make_async_copy(t_hbm, tv, lsem.at[3]),
    ]
    for load in loads[:3]:
        load.start()
    barrier = pltpu.get_barrier_semaphore()
    around = [(1, 0, 0, 0), (-1, 0, 0, 0), (0, 1, 0, 0), (0, -1, 0, 0), (0, 0, 1, 0), (0, 0, -1, 0), (0, 0, 0, 1)]
    for offset in around:
        pl.semaphore_signal(barrier, inc=1, device_id=device(*offset), device_id_type=MESH)

    mine = pl.ds(pl.multiple_of(c * CH, 16), CH)
    own = pl.ds(pl.multiple_of(z * CH, 16), CH)
    below = lax.broadcasted_iota(jnp.int32, (NB, NB), 0) >= lax.broadcasted_iota(jnp.int32, (NB, NB), 1)

    def factor(panel):
        full = dv[panel].astype(jnp.float32)
        lower = jnp.where(below, full, 0.0).astype(jnp.bfloat16)
        block = lax.dot_general(
            pv[:, panel * NB : (panel + 1) * NB], lower, NT, preferred_element_type=jnp.float32
        ).astype(jnp.bfloat16)
        rows[panel][y, x, mine, :] = block
        cols[panel][own, :] = block

    sent = []

    def send(ref, recv_sem, offset):
        copy = pltpu.make_async_remote_copy(
            src_ref=ref,
            dst_ref=ref,
            send_sem=ssem.at[len(sent)],
            recv_sem=recv_sem,
            device_id=device(*offset),
            device_id_type=MESH,
        )
        copy.start()
        sent.append(copy)

    def slot(chunk, mirrored=False):
        panel, dy, dx = chunk
        way, core = (-sign, 1 - c) if mirrored else (sign, c)
        yy = lax.rem(y + way * dy + NY, NY)
        xx = lax.rem(x + way * dx + NX, NX)
        ref = rows[panel].at[yy, xx, pl.ds(pl.multiple_of(core * CH, 16), CH), :]
        return ref, rsem.at[panel * 32 + (yy * NX + xx) * 2 + core]

    def wait(ref, sem):
        pltpu.make_async_remote_copy(
            src_ref=ref, dst_ref=ref, send_sem=ssem.at[0], recv_sem=sem, device_id=device(0, 0, 0, 1), device_id_type=MESH
        ).wait_recv()

    def pass_on(chunk):
        ref, sem = slot(chunk)
        for dy, dx in forwards(chunk):
            send(ref, sem, (0, dy, dx, 0))
        send(ref, sem, (0, 0, 0, 1))

    def zslot(part, dz):
        panel, first = ZPARTS[part]
        zz = lax.rem(z + sign * dz + NZ, NZ)
        ref = cols[panel].at[pl.ds(pl.multiple_of(zz * CH, 16), CH), pl.ds(first, QUARTER)]
        return ref, zsem.at[part * NZ + zz]

    def zstart(part):
        ref, sem = zslot(part, 0)
        for way in (1, -1):
            send(ref, sem, (way, 0, 0, 0))

    def zpass_on(part, hop):
        last_way = 1 if part % 2 == 0 else -1
        for way in (1, -1):
            if hop == NZ // 2 and way != last_way:
                continue
            ref, sem = zslot(part, -way * hop)
            wait(ref, sem)
            if hop + 1 < NZ // 2 or (hop + 1 == NZ // 2 and way == last_way):
                send(ref, sem, (way, 0, 0, 0))

    from_sibling = set()

    def wait_sibling(chunk):
        if chunk not in from_sibling:
            from_sibling.add(chunk)
            wait(*slot(chunk, mirrored=True))

    def other(d):
        return d if d == 2 else -d

    touched = set()

    def chip_at(dy, dx):
        return lax.rem(y + sign * dy + NY, NY), lax.rem(x + sign * dx + NX, NX)

    def update(panel, chips):
        for dy, dx in chips:
            wait_sibling((panel, other(dy), other(dx)))
        for dy, dx in chips:
            yy, xx = chip_at(dy, dx)
            product = lax.dot_general(rows[panel][yy, xx], cols[panel][...], NT, preferred_element_type=jnp.float32)
            before = acc[yy, xx] if (dy, dx) in touched else tv[yy, xx].astype(jnp.float32)
            touched.add((dy, dx))
            acc[yy, xx] = before - product

    loads[0].wait()
    loads[1].wait()
    factor(0)
    pl.semaphore_wait(barrier, len(around))
    pass_on((0, 0, 0))
    zstart(0)
    zstart(1)
    loads[2].wait()
    factor(1)
    pass_on((1, 0, 0))
    zstart(2)
    loads[3].start()
    for what, *arg in PLAN:
        if what == "row":
            for chunk in RECV[arg[0]]:
                wait(*slot(chunk))
                pass_on(chunk)
            if arg[0] == 3:
                loads[3].wait()
                for chip in UNTOUCHED:
                    yy, xx = chip_at(*chip)
                    acc[yy, xx] = tv[yy, xx].astype(jnp.float32)
        elif what == "z":
            zpass_on(*arg)
        elif what == "own":
            zstart(*arg)
        else:
            update(*arg)
    for chunks in [[(0, 0, 0), (1, 0, 0)]] + RECV:
        for chunk in chunks:
            wait_sibling(chunk)
    for copy in sent:
        copy.wait_send()


N_SENDS = 30 + 32 + 7 * len(ZPARTS)


def update_kernel(ra, rb, ca, cb, acc, f_hbm, o_hbm, ob, osem, fsem):
    _, y, x, c = place()
    sign = 1 - 2 * c
    mine = pl.ds(pl.multiple_of(c * CH, 16), CH)
    keep = [
        pltpu.make_async_copy(r.at[y, x, mine, :], f_hbm.at[:, panel * NB : (panel + 1) * NB], fsem.at[panel])
        for panel, r in enumerate((ra, rb))
    ]
    for copy in keep:
        copy.start()

    writes = []
    for i, (dy, dx) in enumerate(CHIPS):
        yy = lax.rem(y + sign * dy + NY, NY)
        xx = lax.rem(x + sign * dx + NX, NX)
        value = acc[yy, xx]
        for panel, (r, cf) in enumerate(((ra, ca), (rb, cb))):
            if (panel, (dy, dx)) not in DONE:
                value -= lax.dot_general(r[yy, xx], cf[...], NT, preferred_element_type=jnp.float32)
        ob[i] = value.astype(jnp.bfloat16)
        copy = pltpu.make_async_copy(ob.at[i], o_hbm.at[yy, xx], osem.at[i])
        copy.start()
        writes.append(copy)
    for copy in writes:
        copy.wait()
    for copy in keep:
        copy.wait()


def body(panel_block, diag_inverse, trailing):
    vmem = pl.BlockSpec(memory_space=pltpu.VMEM)
    hbm = pl.BlockSpec(memory_space=pltpu.HBM)
    bf16 = jnp.bfloat16
    half = jax.ShapeDtypeStruct((NY, NX, PAIR, NB), bf16)
    column = jax.ShapeDtypeStruct((COLS, NB), bf16)
    blocks = (NY, NX, PAIR, COLS)
    inputs = (panel_block, diag_inverse, trailing.reshape(blocks))
    gathered = pl.pallas_call(
        gather_kernel,
        name="gather",
        out_shape=[half, half, column, column, jax.ShapeDtypeStruct(blocks, jnp.float32)],
        in_specs=[hbm] * 3,
        out_specs=[vmem] * 5,
        scratch_shapes=[
            pltpu.VMEM((CH, 2 * NB), bf16),
            pltpu.VMEM((2, NB, NB), bf16),
            pltpu.VMEM(blocks, bf16),
            pltpu.SemaphoreType.DMA((4,)),
            pltpu.SemaphoreType.DMA((N_SENDS,)),
            pltpu.SemaphoreType.DMA((64,)),
            pltpu.SemaphoreType.DMA((NZ * len(ZPARTS),)),
        ],
        compiler_params=pltpu.CompilerParams(
            collective_id=0, has_side_effects=True, vmem_limit_bytes=24 << 20
        ),
    )(*(pltpu.with_memory_space_constraint(a, pltpu.HBM) for a in inputs))
    factor, updated = pl.pallas_call(
        update_kernel,
        name="update",
        out_shape=[
            jax.ShapeDtypeStruct(panel_block.shape, bf16),
            jax.ShapeDtypeStruct(blocks, bf16),
        ],
        in_specs=[vmem] * len(gathered),
        out_specs=[hbm] * 2,
        scratch_shapes=[
            pltpu.VMEM((NY * NX, PAIR, COLS), bf16),
            pltpu.SemaphoreType.DMA((NY * NX,)),
            pltpu.SemaphoreType.DMA((2,)),
        ],
        compiler_params=pltpu.CompilerParams(vmem_limit_bytes=24 << 20),
    )(*gathered)
    return factor, updated.reshape(trailing.shape)


def solution(mesh):
    placed = (P(("row", "col"), None), P(), P("row", "col"))
    return jax.shard_map(
        body,
        mesh=mesh,
        in_specs=placed,
        out_specs=(P(("row", "col"), None), P("row", "col")),
        check_vma=False,
    )
```

```python
import jax
import jax.numpy as jnp
from jax import lax
from jax.experimental import pallas as pl
from jax.experimental.pallas import tpu as pltpu
from jax.sharding import PartitionSpec as P

NB = 512
CH = 112
NZ = 8
NY = 4
NX = 4
PAIR = 2 * CH
COLS = NZ * CH
ROWS = NY * NX * PAIR
QUARTER = NB // 2
LANES = 128
TWO = 2 * LANES
MESH = pl.DeviceIdType.MESH
NT = (((1,), (1,)), ((), ()))

RECV = [
    [(0, 0, -1), (1, -1, 0), (0, 0, 1), (1, 1, 0)],
    [(1, 0, -1), (0, -1, 0), (1, 0, 1), (0, 1, 0)],
    [(0, 0, 2), (1, 2, 0), (0, 1, -1), (1, -1, 1)],
    [(0, -1, -1), (1, -1, -1), (0, 1, 1), (1, 1, 1)],
    [(0, -1, 1), (1, 1, -1), (0, 1, 2), (1, 2, 1)],
    [(0, 2, 0), (1, 0, 2), (0, 2, -1), (1, -1, 2)],
    [(0, -1, 2), (1, 2, -1), (0, 2, 2), (1, 2, 2)],
    [(0, 2, 1), (1, 1, 2)],
]
ZPARTS = [(0, 0), (0, QUARTER), (1, 0), (1, QUARTER)]
CROSS = [(0, 0), (0, -1), (0, 1), (-1, 0), (1, 0)]
CORNERS = [(1, -1), (1, 1), (-1, -1), (-1, 1)]
ENDS = [(0, 2), (2, 0)]
PLAN = [
    ("own", 3),
    ("z", 0, 1),
    ("z", 1, 1),
    ("row", 0),
    ("z", 2, 1),
    ("z", 3, 1),
    ("row", 1),
    ("do", 1, CROSS),
    ("z", 0, 2),
    ("z", 1, 2),
    ("row", 2),
    ("z", 2, 2),
    ("z", 3, 2),
    ("row", 3),
    ("do", 2, CROSS),
    ("z", 0, 3),
    ("z", 1, 3),
    ("row", 4),
    ("do", 1, CORNERS),
    ("z", 2, 3),
    ("z", 3, 3),
    ("do", 2, CORNERS),
    ("row", 5),
    ("do", 3, CROSS),
    ("do", 1, ENDS),
    ("do", 2, ENDS),
    ("z", 0, 4),
    ("z", 1, 4),
    ("do", 3, CORNERS),
    ("row", 6),
    ("z", 2, 4),
    ("z", 3, 4),
    ("do", 4, CROSS),
    ("row", 7),
    ("do", 3, ENDS),
    ("do", 4, CORNERS),
    ("do", 4, ENDS),
]
READY = CROSS + CORNERS + ENDS
OPEN = [(dy, dx) for dy in (2, -1, 1, 0) for dx in (2, -1, 1, 0) if (dy, dx) not in READY]
CHIPS = [chip for k, first in enumerate(OPEN) for chip in [first, *READY[2 * k : 2 * k + 2]]] + READY[2 * len(OPEN) :]


def place():
    j = lax.axis_index("col")
    return lax.axis_index("row"), lax.div(j, 8), lax.rem(lax.div(j, 2), NX), lax.rem(j, 2)


def forwards(chunk):
    panel, dy, dx = chunk
    near, far = (dx, dy) if panel == 0 else (dy, dx)
    steps = []
    if far == 0:
        if near == 0:
            steps += [("near", 1), ("near", -1)]
        elif near == -1:
            steps += [("near", 1)]
        steps += [("far", 1), ("far", -1)]
    elif far == -1 and near in (0, 1):
        steps += [("far", 1)]
    elif far == 1 and near in (-1, 2):
        steps += [("far", -1)]
    axis = {"near": 1 - panel, "far": panel}
    return [(0, d) if axis[kind] == 1 else (d, 0) for kind, d in steps]


def gather_kernel(panel_hbm, diag_hbm, t_hbm, ra, rb, ca, cb, acc, tv, pv, dv, lsem, ssem, rsem, zsem):
    z, y, x, c = place()
    sign = 1 - 2 * c
    rows = (ra, rb)
    cols = (ca, cb)

    def device(dz, dy, dx, dc):
        zz = lax.rem(z + sign * dz + NZ, NZ)
        yy = lax.rem(y + sign * dy + NY, NY)
        xx = lax.rem(x + sign * dx + NX, NX)
        cc = 1 - c if dc else c
        return (zz, (yy * NX + xx) * 2 + cc)

    loads = [
        pltpu.make_async_copy(panel_hbm, pv, lsem.at[0]),
        pltpu.make_async_copy(diag_hbm.at[0], dv.at[0], lsem.at[1]),
        pltpu.make_async_copy(diag_hbm.at[1], dv.at[1], lsem.at[2]),
        pltpu.make_async_copy(t_hbm, tv, lsem.at[3]),
    ]
    for load in loads[:3]:
        load.start()
    barrier = pltpu.get_barrier_semaphore()
    around = [(1, 0, 0, 0), (-1, 0, 0, 0), (0, 1, 0, 0), (0, -1, 0, 0), (0, 0, 1, 0), (0, 0, -1, 0), (0, 0, 0, 1)]
    for offset in around:
        pl.semaphore_signal(barrier, inc=1, device_id=device(*offset), device_id_type=MESH)

    mine = pl.ds(pl.multiple_of(c * CH, 16), CH)
    own = pl.ds(pl.multiple_of(z * LANES, LANES), CH)
    for cf in cols:
        for k in range(NZ):
            cf[k * LANES + CH : (k + 1) * LANES, :] = jnp.zeros((LANES - CH, NB), jnp.bfloat16)
    below = lax.broadcasted_iota(jnp.int32, (NB, NB), 0) >= lax.broadcasted_iota(jnp.int32, (NB, NB), 1)

    def factor(panel):
        full = dv[panel].astype(jnp.float32)
        lower = jnp.where(below, full, 0.0).astype(jnp.bfloat16)
        block = lax.dot_general(
            pv[:, panel * NB : (panel + 1) * NB], lower, NT, preferred_element_type=jnp.float32
        ).astype(jnp.bfloat16)
        rows[panel][y, x, mine, :] = block
        cols[panel][own, :] = block

    sent = []

    def send(ref, recv_sem, offset):
        copy = pltpu.make_async_remote_copy(
            src_ref=ref,
            dst_ref=ref,
            send_sem=ssem.at[len(sent)],
            recv_sem=recv_sem,
            device_id=device(*offset),
            device_id_type=MESH,
        )
        copy.start()
        sent.append(copy)

    def slot(chunk, mirrored=False):
        panel, dy, dx = chunk
        way, core = (-sign, 1 - c) if mirrored else (sign, c)
        yy = lax.rem(y + way * dy + NY, NY)
        xx = lax.rem(x + way * dx + NX, NX)
        ref = rows[panel].at[yy, xx, pl.ds(pl.multiple_of(core * CH, 16), CH), :]
        return ref, rsem.at[panel * 32 + (yy * NX + xx) * 2 + core]

    def wait(ref, sem):
        pltpu.make_async_remote_copy(
            src_ref=ref, dst_ref=ref, send_sem=ssem.at[0], recv_sem=sem, device_id=device(0, 0, 0, 1), device_id_type=MESH
        ).wait_recv()

    def pass_on(chunk):
        ref, sem = slot(chunk)
        for dy, dx in forwards(chunk):
            send(ref, sem, (0, dy, dx, 0))
        send(ref, sem, (0, 0, 0, 1))

    def zslot(part, dz):
        panel, first = ZPARTS[part]
        zz = lax.rem(z + sign * dz + NZ, NZ)
        ref = cols[panel].at[pl.ds(pl.multiple_of(zz * LANES, LANES), CH), pl.ds(first, QUARTER)]
        return ref, zsem.at[part * NZ + zz]

    def zstart(part):
        ref, sem = zslot(part, 0)
        for way in (1, -1):
            send(ref, sem, (way, 0, 0, 0))

    def zpass_on(part, hop):
        last_way = 1 if part % 2 == 0 else -1
        for way in (1, -1):
            if hop == NZ // 2 and way != last_way:
                continue
            ref, sem = zslot(part, -way * hop)
            wait(ref, sem)
            if hop + 1 < NZ // 2 or (hop + 1 == NZ // 2 and way == last_way):
                send(ref, sem, (way, 0, 0, 0))

    from_sibling = set()

    def wait_sibling(chunk):
        if chunk not in from_sibling:
            from_sibling.add(chunk)
            wait(*slot(chunk, mirrored=True))

    def other(d):
        return d if d == 2 else -d

    def update(hops, chips):
        side = 1 - 2 * lax.rem(z, 2)
        at = lax.rem(z + side * (hops if hops % 2 == 1 else -hops) + NZ, NZ)
        lanes = pl.ds(pl.multiple_of(lax.div(at, 2) * TWO, TWO), TWO)
        for dy, dx in chips:
            for panel in range(2):
                wait_sibling((panel, other(dy), other(dx)))
        for dy, dx in chips:
            yy = lax.rem(y + sign * dy + NY, NY)
            xx = lax.rem(x + sign * dx + NX, NX)
            product = lax.dot_general(ra[yy, xx], ca[lanes, :], NT, preferred_element_type=jnp.float32)
            product += lax.dot_general(rb[yy, xx], cb[lanes, :], NT, preferred_element_type=jnp.float32)
            acc[yy, xx, :, lanes] = product

    loads[0].wait()
    loads[1].wait()
    factor(0)
    pl.semaphore_wait(barrier, len(around))
    pass_on((0, 0, 0))
    zstart(0)
    zstart(1)
    loads[2].wait()
    factor(1)
    pass_on((1, 0, 0))
    zstart(2)
    loads[3].start()
    for what, *arg in PLAN:
        if what == "row":
            for chunk in RECV[arg[0]]:
                wait(*slot(chunk))
                pass_on(chunk)
        elif what == "z":
            zpass_on(*arg)
        elif what == "own":
            zstart(*arg)
        else:
            update(*arg)
    for chunks in [[(0, 0, 0), (1, 0, 0)]] + RECV:
        for chunk in chunks:
            wait_sibling(chunk)
    for copy in sent:
        copy.wait_send()
    loads[3].wait()


N_SENDS = 30 + 32 + 7 * len(ZPARTS)


def update_kernel(ra, rb, ca, cb, acc, tv, f_hbm, o_hbm, ob, osem, fsem):
    _, y, x, c = place()
    sign = 1 - 2 * c
    mine = pl.ds(pl.multiple_of(c * CH, 16), CH)
    keep = [
        pltpu.make_async_copy(r.at[y, x, mine, :], f_hbm.at[:, panel * NB : (panel + 1) * NB], fsem.at[panel])
        for panel, r in enumerate((ra, rb))
    ]
    for copy in keep:
        copy.start()

    writes = []
    for i, (dy, dx) in enumerate(CHIPS):
        yy = lax.rem(y + sign * dy + NY, NY)
        xx = lax.rem(x + sign * dx + NX, NX)
        if (dy, dx) in READY:
            product = acc[yy, xx]
        else:
            product = lax.dot_general(ra[yy, xx], ca[...], NT, preferred_element_type=jnp.float32)
            product += lax.dot_general(rb[yy, xx], cb[...], NT, preferred_element_type=jnp.float32)
        product = jnp.concatenate([product[:, k * LANES : k * LANES + CH] for k in range(NZ)], axis=1)
        ob[i] = (tv[yy, xx].astype(jnp.float32) - product).astype(jnp.bfloat16)
        copy = pltpu.make_async_copy(ob.at[i], o_hbm.at[yy, xx], osem.at[i])
        copy.start()
        writes.append(copy)
    for copy in writes:
        copy.wait()
    for copy in keep:
        copy.wait()


def body(panel_block, diag_inverse, trailing):
    vmem = pl.BlockSpec(memory_space=pltpu.VMEM)
    hbm = pl.BlockSpec(memory_space=pltpu.HBM)
    bf16 = jnp.bfloat16
    half = jax.ShapeDtypeStruct((NY, NX, PAIR, NB), bf16)
    column = jax.ShapeDtypeStruct((NZ * LANES, NB), bf16)
    blocks = (NY, NX, PAIR, COLS)
    inputs = (panel_block, diag_inverse, trailing.reshape(blocks))
    gathered = pl.pallas_call(
        gather_kernel,
        name="gather",
        out_shape=[
            half,
            half,
            column,
            column,
            jax.ShapeDtypeStruct((NY, NX, PAIR, NZ * LANES), jnp.float32),
            jax.ShapeDtypeStruct(blocks, bf16),
        ],
        in_specs=[hbm] * 3,
        out_specs=[vmem] * 6,
        scratch_shapes=[
            pltpu.VMEM((CH, 2 * NB), bf16),
            pltpu.VMEM((2, NB, NB), bf16),
            pltpu.SemaphoreType.DMA((4,)),
            pltpu.SemaphoreType.DMA((N_SENDS,)),
            pltpu.SemaphoreType.DMA((64,)),
            pltpu.SemaphoreType.DMA((NZ * len(ZPARTS),)),
        ],
        compiler_params=pltpu.CompilerParams(
            collective_id=0, has_side_effects=True, vmem_limit_bytes=20 << 20
        ),
    )(*(pltpu.with_memory_space_constraint(a, pltpu.HBM) for a in inputs))
    factor, updated = pl.pallas_call(
        update_kernel,
        name="update",
        out_shape=[
            jax.ShapeDtypeStruct(panel_block.shape, bf16),
            jax.ShapeDtypeStruct(blocks, bf16),
        ],
        in_specs=[vmem] * len(gathered),
        out_specs=[hbm] * 2,
        scratch_shapes=[
            pltpu.VMEM((NY * NX, PAIR, COLS), bf16),
            pltpu.SemaphoreType.DMA((NY * NX,)),
            pltpu.SemaphoreType.DMA((2,)),
        ],
        compiler_params=pltpu.CompilerParams(vmem_limit_bytes=20 << 20),
    )(*gathered)
    return factor, updated.reshape(trailing.shape)


def solution(mesh):
    placed = (P(("row", "col"), None), P(), P("row", "col"))
    return jax.shard_map(
        body,
        mesh=mesh,
        in_specs=placed,
        out_specs=(P(("row", "col"), None), P("row", "col")),
        check_vma=False,
    )
```

```python
import jax
import jax.numpy as jnp
from jax import lax
from jax.experimental import pallas as pl
from jax.experimental.pallas import tpu as pltpu
from jax.sharding import PartitionSpec as P

NB = 512
CH = 112
NZ = 8
NY = 4
NX = 4
PAIR = 2 * CH
COLS = NZ * CH
ROWS = NY * NX * PAIR
WIDTH = NB
LANES = 128
TWO = 2 * LANES
MESH = pl.DeviceIdType.MESH
NT = (((1,), (1,)), ((), ()))

RECV = [
    [(0, 0, -1), (1, -1, 0), (0, 0, 1), (1, 1, 0)],
    [(1, 0, -1), (0, -1, 0), (1, 0, 1), (0, 1, 0)],
    [(0, 0, 2), (1, 2, 0), (0, 1, -1), (1, -1, 1)],
    [(0, -1, -1), (1, -1, -1), (0, 1, 1), (1, 1, 1)],
    [(0, -1, 1), (1, 1, -1), (0, 1, 2), (1, 2, 1)],
    [(0, 2, 0), (1, 0, 2), (0, 2, -1), (1, -1, 2)],
    [(0, -1, 2), (1, 2, -1), (0, 2, 2), (1, 2, 2)],
    [(0, 2, 1), (1, 1, 2)],
]
ZPARTS = [(0, 0), (1, 0)]
CROSS = [(0, 0), (0, -1), (0, 1), (-1, 0), (1, 0)]
CORNERS = [(1, -1), (1, 1), (-1, -1), (-1, 1)]
ENDS = [(0, 2), (2, 0)]
PLAN = [
    ("z", 0, 1),
    ("row", 0),
    ("z", 1, 1),
    ("row", 1),
    ("do", 1, CROSS),
    ("z", 0, 2),
    ("row", 2),
    ("z", 1, 2),
    ("row", 3),
    ("do", 2, CROSS),
    ("z", 0, 3),
    ("row", 4),
    ("do", 1, CORNERS),
    ("z", 1, 3),
    ("do", 2, CORNERS),
    ("row", 5),
    ("do", 3, CROSS),
    ("do", 1, ENDS),
    ("do", 2, ENDS),
    ("z", 0, 4),
    ("do", 3, CORNERS),
    ("row", 6),
    ("z", 1, 4),
    ("do", 4, CROSS),
    ("row", 7),
    ("do", 3, ENDS),
    ("do", 4, CORNERS),
    ("do", 4, ENDS),
]
READY = CROSS + CORNERS + ENDS
OPEN = [(dy, dx) for dy in (2, -1, 1, 0) for dx in (2, -1, 1, 0) if (dy, dx) not in READY]
CHIPS = [chip for k, first in enumerate(OPEN) for chip in [first, *READY[2 * k : 2 * k + 2]]] + READY[2 * len(OPEN) :]


def place():
    j = lax.axis_index("col")
    return lax.axis_index("row"), lax.div(j, 8), lax.rem(lax.div(j, 2), NX), lax.rem(j, 2)


def forwards(chunk):
    panel, dy, dx = chunk
    near, far = (dx, dy) if panel == 0 else (dy, dx)
    steps = []
    if far == 0:
        if near == 0:
            steps += [("near", 1), ("near", -1)]
        elif near == -1:
            steps += [("near", 1)]
        steps += [("far", 1), ("far", -1)]
    elif far == -1 and near in (0, 1):
        steps += [("far", 1)]
    elif far == 1 and near in (-1, 2):
        steps += [("far", -1)]
    axis = {"near": 1 - panel, "far": panel}
    return [(0, d) if axis[kind] == 1 else (d, 0) for kind, d in steps]


def gather_kernel(panel_hbm, diag_hbm, t_hbm, ra, rb, ca, cb, acc, tv, pv, dv, lsem, ssem, rsem, zsem):
    z, y, x, c = place()
    sign = 1 - 2 * c
    rows = (ra, rb)
    cols = (ca, cb)

    def device(dz, dy, dx, dc):
        zz = lax.rem(z + sign * dz + NZ, NZ)
        yy = lax.rem(y + sign * dy + NY, NY)
        xx = lax.rem(x + sign * dx + NX, NX)
        cc = 1 - c if dc else c
        return (zz, (yy * NX + xx) * 2 + cc)

    loads = [
        pltpu.make_async_copy(panel_hbm, pv, lsem.at[0]),
        pltpu.make_async_copy(diag_hbm.at[0], dv.at[0], lsem.at[1]),
        pltpu.make_async_copy(diag_hbm.at[1], dv.at[1], lsem.at[2]),
        pltpu.make_async_copy(t_hbm, tv, lsem.at[3]),
    ]
    for load in loads[:3]:
        load.start()
    barrier = pltpu.get_barrier_semaphore()
    around = [(1, 0, 0, 0), (-1, 0, 0, 0), (0, 1, 0, 0), (0, -1, 0, 0), (0, 0, 1, 0), (0, 0, -1, 0), (0, 0, 0, 1)]
    for offset in around:
        pl.semaphore_signal(barrier, inc=1, device_id=device(*offset), device_id_type=MESH)

    mine = pl.ds(pl.multiple_of(c * CH, 16), CH)
    own = pl.ds(pl.multiple_of(z * LANES, LANES), CH)
    for cf in cols:
        for k in range(NZ):
            cf[k * LANES + CH : (k + 1) * LANES, :] = jnp.zeros((LANES - CH, NB), jnp.bfloat16)
    below = lax.broadcasted_iota(jnp.int32, (NB, NB), 0) >= lax.broadcasted_iota(jnp.int32, (NB, NB), 1)

    def factor(panel):
        full = dv[panel].astype(jnp.float32)
        lower = jnp.where(below, full, 0.0).astype(jnp.bfloat16)
        block = lax.dot_general(
            pv[:, panel * NB : (panel + 1) * NB], lower, NT, preferred_element_type=jnp.float32
        ).astype(jnp.bfloat16)
        rows[panel][y, x, mine, :] = block
        cols[panel][own, :] = block

    sent = []

    def send(ref, recv_sem, offset):
        copy = pltpu.make_async_remote_copy(
            src_ref=ref,
            dst_ref=ref,
            send_sem=ssem.at[len(sent)],
            recv_sem=recv_sem,
            device_id=device(*offset),
            device_id_type=MESH,
        )
        copy.start()
        sent.append(copy)

    def slot(chunk, mirrored=False):
        panel, dy, dx = chunk
        way, core = (-sign, 1 - c) if mirrored else (sign, c)
        yy = lax.rem(y + way * dy + NY, NY)
        xx = lax.rem(x + way * dx + NX, NX)
        ref = rows[panel].at[yy, xx, pl.ds(pl.multiple_of(core * CH, 16), CH), :]
        return ref, rsem.at[panel * 32 + (yy * NX + xx) * 2 + core]

    def wait(ref, sem):
        pltpu.make_async_remote_copy(
            src_ref=ref, dst_ref=ref, send_sem=ssem.at[0], recv_sem=sem, device_id=device(0, 0, 0, 1), device_id_type=MESH
        ).wait_recv()

    def pass_on(chunk):
        ref, sem = slot(chunk)
        for dy, dx in forwards(chunk):
            send(ref, sem, (0, dy, dx, 0))
        send(ref, sem, (0, 0, 0, 1))

    def zslot(part, dz):
        panel, first = ZPARTS[part]
        zz = lax.rem(z + sign * dz + NZ, NZ)
        ref = cols[panel].at[pl.ds(pl.multiple_of(zz * LANES, LANES), CH), pl.ds(first, WIDTH)]
        return ref, zsem.at[part * NZ + zz]

    def zstart(part):
        ref, sem = zslot(part, 0)
        for way in (1, -1):
            send(ref, sem, (way, 0, 0, 0))

    def zpass_on(part, hop):
        last_way = 1 if part % 2 == 0 else -1
        for way in (1, -1):
            if hop == NZ // 2 and way != last_way:
                continue
            ref, sem = zslot(part, -way * hop)
            wait(ref, sem)
            if hop + 1 < NZ // 2 or (hop + 1 == NZ // 2 and way == last_way):
                send(ref, sem, (way, 0, 0, 0))

    from_sibling = set()

    def wait_sibling(chunk):
        if chunk not in from_sibling:
            from_sibling.add(chunk)
            wait(*slot(chunk, mirrored=True))

    def other(d):
        return d if d == 2 else -d

    def update(hops, chips):
        side = 1 - 2 * lax.rem(z, 2)
        at = lax.rem(z + side * (hops if hops % 2 == 1 else -hops) + NZ, NZ)
        lanes = pl.ds(pl.multiple_of(lax.div(at, 2) * TWO, TWO), TWO)
        for dy, dx in chips:
            for panel in range(2):
                wait_sibling((panel, other(dy), other(dx)))
        for dy, dx in chips:
            yy = lax.rem(y + sign * dy + NY, NY)
            xx = lax.rem(x + sign * dx + NX, NX)
            product = lax.dot_general(ra[yy, xx], ca[lanes, :], NT, preferred_element_type=jnp.float32)
            product += lax.dot_general(rb[yy, xx], cb[lanes, :], NT, preferred_element_type=jnp.float32)
            acc[yy, xx, :, lanes] = product

    loads[0].wait()
    loads[1].wait()
    factor(0)
    pl.semaphore_wait(barrier, len(around))
    pass_on((0, 0, 0))
    zstart(0)
    loads[2].wait()
    factor(1)
    pass_on((1, 0, 0))
    zstart(1)
    loads[3].start()
    for what, *arg in PLAN:
        if what == "row":
            for chunk in RECV[arg[0]]:
                wait(*slot(chunk))
                pass_on(chunk)
        elif what == "z":
            zpass_on(*arg)
        else:
            update(*arg)
    for chunks in [[(0, 0, 0), (1, 0, 0)]] + RECV:
        for chunk in chunks:
            wait_sibling(chunk)
    for copy in sent:
        copy.wait_send()
    loads[3].wait()


N_SENDS = 30 + 32 + 7 * len(ZPARTS)


def update_kernel(ra, rb, ca, cb, acc, tv, f_hbm, o_hbm, ob, osem, fsem):
    _, y, x, c = place()
    sign = 1 - 2 * c
    mine = pl.ds(pl.multiple_of(c * CH, 16), CH)
    keep = [
        pltpu.make_async_copy(r.at[y, x, mine, :], f_hbm.at[:, panel * NB : (panel + 1) * NB], fsem.at[panel])
        for panel, r in enumerate((ra, rb))
    ]
    for copy in keep:
        copy.start()

    writes = []
    for i, (dy, dx) in enumerate(CHIPS):
        yy = lax.rem(y + sign * dy + NY, NY)
        xx = lax.rem(x + sign * dx + NX, NX)
        if (dy, dx) in READY:
            product = acc[yy, xx]
        else:
            product = lax.dot_general(ra[yy, xx], ca[...], NT, preferred_element_type=jnp.float32)
            product += lax.dot_general(rb[yy, xx], cb[...], NT, preferred_element_type=jnp.float32)
        product = jnp.concatenate([product[:, k * LANES : k * LANES + CH] for k in range(NZ)], axis=1)
        ob[i] = (tv[yy, xx].astype(jnp.float32) - product).astype(jnp.bfloat16)
        copy = pltpu.make_async_copy(ob.at[i], o_hbm.at[yy, xx], osem.at[i])
        copy.start()
        writes.append(copy)
    for copy in writes:
        copy.wait()
    for copy in keep:
        copy.wait()


def body(panel_block, diag_inverse, trailing):
    vmem = pl.BlockSpec(memory_space=pltpu.VMEM)
    hbm = pl.BlockSpec(memory_space=pltpu.HBM)
    bf16 = jnp.bfloat16
    half = jax.ShapeDtypeStruct((NY, NX, PAIR, NB), bf16)
    column = jax.ShapeDtypeStruct((NZ * LANES, NB), bf16)
    blocks = (NY, NX, PAIR, COLS)
    inputs = (panel_block, diag_inverse, trailing.reshape(blocks))
    gathered = pl.pallas_call(
        gather_kernel,
        name="gather",
        out_shape=[
            half,
            half,
            column,
            column,
            jax.ShapeDtypeStruct((NY, NX, PAIR, NZ * LANES), jnp.float32),
            jax.ShapeDtypeStruct(blocks, bf16),
        ],
        in_specs=[hbm] * 3,
        out_specs=[vmem] * 6,
        scratch_shapes=[
            pltpu.VMEM((CH, 2 * NB), bf16),
            pltpu.VMEM((2, NB, NB), bf16),
            pltpu.SemaphoreType.DMA((4,)),
            pltpu.SemaphoreType.DMA((N_SENDS,)),
            pltpu.SemaphoreType.DMA((64,)),
            pltpu.SemaphoreType.DMA((NZ * len(ZPARTS),)),
        ],
        compiler_params=pltpu.CompilerParams(
            collective_id=0, has_side_effects=True, vmem_limit_bytes=20 << 20
        ),
    )(*(pltpu.with_memory_space_constraint(a, pltpu.HBM) for a in inputs))
    factor, updated = pl.pallas_call(
        update_kernel,
        name="update",
        out_shape=[
            jax.ShapeDtypeStruct(panel_block.shape, bf16),
            jax.ShapeDtypeStruct(blocks, bf16),
        ],
        in_specs=[vmem] * len(gathered),
        out_specs=[hbm] * 2,
        scratch_shapes=[
            pltpu.VMEM((NY * NX, PAIR, COLS), bf16),
            pltpu.SemaphoreType.DMA((NY * NX,)),
            pltpu.SemaphoreType.DMA((2,)),
        ],
        compiler_params=pltpu.CompilerParams(vmem_limit_bytes=20 << 20),
    )(*gathered)
    return factor, updated.reshape(trailing.shape)


def solution(mesh):
    placed = (P(("row", "col"), None), P(), P("row", "col"))
    return jax.shard_map(
        body,
        mesh=mesh,
        in_specs=placed,
        out_specs=(P(("row", "col"), None), P("row", "col")),
        check_vma=False,
    )
```
